32 devices in a mesh: seq: 8 (over z, x), kvh: 2 (over core), batch: 2 (over y).
Axes of the slice: x: 2, y: 2, z: 4, core: 2. Of those that a mesh axis runs over, the one named last changes fastest.
Arguments:
- queries: bfloat16 [8, 512, 3584], P('batch', 'seq', 'kvh'), parts along dimension 0, may hold values from -160 to 160
- text_keys: bfloat16 [8, 512, 512], P('batch', 'seq', 'kvh'), parts along dimension 0, may hold values from -6 to 6
- text_values: bfloat16 [8, 512, 512], P('batch', 'seq', 'kvh'), parts along dimension 0, may hold values from -6 to 6
- visual_keys: bfloat16 [32, 729, 512], P(('batch', 'seq'), None, 'kvh'), parts along dimension 0, may hold values from -6 to 6
- visual_values: bfloat16 [32, 729, 512], P(('batch', 'seq'), None, 'kvh'), parts along dimension 0, may hold values from -6 to 6
- gate_weight: float32 [3584, 28], P('kvh'), may hold values from -0.1875 to 0.1875
- text_offsets: int32 [16], P('batch'), parts along dimension 0, may hold values from 0 to 448, as said below
- image_sequence: int32 [32], P('batch'), parts along dimension 0, may hold values from 0 to 3, as said below
- image_position: int32 [32], P('batch'), parts along dimension 0, may hold values from 0 to 511, as said below
Outputs:
- combined: bfloat16 [8, 512, 3584], P('batch', 'seq', 'kvh'), parts along dimension 0
The draws below stay inside these ranges and needn't reach their ends.
There are 2 independent parts, one for each index of `batch`. The reference program is written for one: setup_inputs(seed, part) draws one part's arguments, and reference() takes and returns one part's arrays. A program takes and returns all parts, laid end to end along the dimension named above; an argument that names none is the same for every part. Nothing has to cross between parts.
Inputs may be any that keep to these rules, and one draw needn't show every extreme that they name: A permutation of the multiples of 64 below 512: text block j holds the positions text_offsets[j] to text_offsets[j] + 63. `image_sequence`: each of the 4 sequences owns exactly 4 images. `image_position`: every sequence has an image at position 0.
All inputs are finite; a program needn't handle non-finite values.
Results may differ from the reference program's by a relative error of at most 0.0039.
Values may be sent and summed in bfloat16 or wider, within the bound.
A program may use at most 128 MiB of HBM per device.

```python
import jax
import jax.numpy as jnp
from jax import lax

HQ = 28
KVH = 4
DH = 128
VTOK = 729
TOK_DEV = 64
SEQS = 4
IMG_SEQ = 4
GROUP = 7
SHARDS = 8
L = 512
IMAGES = 16


def layout_order(key):
    return jax.random.permutation(jax.random.fold_in(key, 101), SHARDS).astype(jnp.int32)


def image_plan(key):
    shuffled = jax.random.permutation(jax.random.fold_in(key, 202), IMAGES).astype(jnp.int32)
    owners = (shuffled % SEQS).astype(jnp.int32)
    places = jax.random.randint(jax.random.fold_in(key, 203), (IMAGES,), 1, L, dtype=jnp.int32)
    places = jnp.where(shuffled < SEQS, 0, places).astype(jnp.int32)
    return (owners, places)


def text_key_base(key):
    return jnp.clip(jax.random.normal(jax.random.fold_in(key, 11), (SEQS, L, KVH * DH), jnp.float32), -6.0, 6.0)


def visual_key_base(key):
    return jnp.clip(jax.random.normal(jax.random.fold_in(key, 12), (IMAGES, VTOK, KVH * DH), jnp.float32), -6.0, 6.0)


def draw_text_offsets(key, part):
    return (layout_order(key) * TOK_DEV).astype(jnp.int32)


def draw_image_sequence(key, part):
    return image_plan(key)[0]


def draw_image_position(key, part):
    return image_plan(key)[1]


def draw_text_keys(key, part):
    drawn = text_key_base(key)
    return drawn.astype(jnp.bfloat16)


def draw_visual_keys(key, part):
    drawn = visual_key_base(key)
    return drawn.astype(jnp.bfloat16)


def draw_queries(key, part):
    drawn = jnp.clip(jax.random.normal(jax.random.fold_in(key, 13), (SEQS, L, HQ * DH), jnp.float32), -6.0, 6.0)
    return drawn.astype(jnp.bfloat16)


def steps_of(rng, dims, cuts, smallest, largest):
    level, own = 1.0, jax.random.fold_in(rng, 6)
    for dim, blocks in cuts:
        draws = jnp.exp(jax.random.uniform(jax.random.fold_in(own, dim), (blocks,), jnp.float32, smallest / len(cuts), largest / len(cuts)))
        level = level * jnp.repeat(draws, dims[dim] // blocks).reshape([-1 if axis == dim else 1 for axis in range(len(dims))])
    return level


def gaussian(own_key, extent, width, bound, pieces=(), kind=jnp.bfloat16):
    values = width * jax.random.normal(own_key, extent, jnp.float32)
    if pieces:
        values = values * steps_of(own_key, extent, pieces, -0.22, 0.18)
    return jnp.clip(values, -bound, bound).astype(kind)


def setup_inputs(seed: int = 0, part: int = 0) -> dict:
    arg_keys = jax.random.split(jax.random.key(seed), 10)
    part_splits = jax.random.split(jax.random.fold_in(arg_keys[9], part), 10)
    return {
        "queries": draw_queries(jax.random.fold_in(jax.random.fold_in(arg_keys[9], part), 71), part),
        "text_keys": draw_text_keys(jax.random.fold_in(jax.random.fold_in(arg_keys[9], part), 71), part),
        "text_values": gaussian(part_splits[2], (SEQS, L, KVH * DH), 1.0, 6.0, ((1, 8), (2, 2))),
        "visual_keys": draw_visual_keys(jax.random.fold_in(jax.random.fold_in(arg_keys[9], part), 71), part),
        "visual_values": gaussian(part_splits[4], (IMAGES, VTOK, KVH * DH), 1.0, 6.0, ((0, 8), (2, 2))),
        "gate_weight": gaussian(arg_keys[5], (HQ * DH, HQ), (HQ * DH // 4) ** -0.5, 0.1875, ((0, 2),), jnp.float32),
        "text_offsets": draw_text_offsets(jax.random.fold_in(jax.random.fold_in(arg_keys[9], part), 71), part),
        "image_sequence": draw_image_sequence(jax.random.fold_in(jax.random.fold_in(arg_keys[9], part), 71), part),
        "image_position": draw_image_position(jax.random.fold_in(jax.random.fold_in(arg_keys[9], part), 71), part),
    }


NEG = -1.0e30


def block_stats(query_rows, key_blocks, value_blocks, visible):
    scaling = 1.0 / (query_rows.shape[-1] ** 0.5)
    scores = jnp.einsum("tghe,bkge->tghbk", query_rows.astype(jnp.float32), key_blocks.astype(jnp.float32), precision=lax.Precision.HIGHEST) * scaling
    allowed = visible[:, None, None, :, :]
    scores = jnp.where(allowed, scores, NEG)
    block_peak = jnp.max(scores, axis=-1)
    unnormed = jnp.where(allowed, jnp.exp(scores - block_peak[..., None]), 0.0)
    block_total = jnp.sum(unnormed, axis=-1)
    rounded = lax.optimization_barrier(unnormed.astype(jnp.bfloat16)).astype(jnp.float32)
    block_sum = jnp.einsum("tghbk,bkge->tghbe", rounded, value_blocks.astype(jnp.float32), precision=lax.Precision.HIGHEST)
    return block_peak, block_total, block_sum


def finish(block_peak, block_total, block_sum):
    overall = jnp.max(block_peak, axis=-1)
    weights = jnp.exp(block_peak - overall[..., None])
    numerator = jnp.sum(weights[..., None] * block_sum, axis=-2)
    denominator = jnp.sum(weights * block_total, axis=-1)
    return numerator / denominator[..., None]


def reference(queries, text_keys, text_values, visual_keys, visual_values, gate_weight, text_offsets, image_sequence, image_position):
    length = queries.shape[1]
    shaped = queries.reshape(SEQS, length, KVH, GROUP, DH)
    rows_all = jnp.arange(length, dtype=jnp.int32)
    positions = (text_offsets[rows_all // TOK_DEV] + rows_all % TOK_DEV).astype(jnp.int32)
    gate_logits = jnp.dot(queries.astype(jnp.float32).reshape(SEQS * length, HQ * DH), gate_weight, precision=lax.Precision.HIGHEST)
    gate = jax.nn.sigmoid(gate_logits).reshape(SEQS, length, KVH, GROUP)
    key_pos = (text_offsets[:, None] + jnp.arange(TOK_DEV, dtype=jnp.int32)[None, :]).astype(jnp.int32)
    text_visible = key_pos[None, :, :] <= positions[:, None, None]
    key_blocks = text_keys.reshape(SEQS, SHARDS, TOK_DEV, KVH, DH)
    value_blocks = text_values.reshape(SEQS, SHARDS, TOK_DEV, KVH, DH)

    def text_one(members):
        query_rows, keys_here, values_here = members
        return finish(*block_stats(query_rows, keys_here, values_here, text_visible))

    text_out = lax.map(text_one, (shaped, key_blocks, value_blocks))
    order = jnp.argsort(image_sequence, stable=True).reshape(SEQS, IMG_SEQ)
    image_keys = visual_keys.reshape(IMAGES, VTOK, KVH, DH)[order]
    image_values = visual_values.reshape(IMAGES, VTOK, KVH, DH)[order]
    image_places = image_position[order]

    def visual_one(members):
        query_rows, keys_here, values_here, places_here = members
        visible = jnp.broadcast_to(places_here[None, :, None] <= positions[:, None, None], (length, IMG_SEQ, VTOK))
        return finish(*block_stats(query_rows, keys_here, values_here, visible))

    visual_out = lax.map(visual_one, (shaped, image_keys, image_values, image_places))
    mixed = (1.0 - gate)[..., None] * text_out + gate[..., None] * visual_out
    return mixed.reshape(SEQS, length, HQ * DH).astype(jnp.bfloat16)
```

```python
import functools

import jax
import jax.numpy as jnp
from jax import lax
from jax.experimental import pallas as pl
from jax.experimental.pallas import tpu as pltpu
from jax.sharding import PartitionSpec as P

DH = 128
GROUP = 7
LANES = 128
HALF = LANES // 2
NEG = -1e30
FAR = 1 << 30


def stack_heads(block):
    return jnp.concatenate([block[:, h * DH:(h + 1) * DH] for h in range(GROUP)], axis=0)


def pack_stats(peak, total, rows):
    lane = lax.broadcasted_iota(jnp.int32, (rows, LANES), 1)
    packed = jnp.zeros((rows, LANES), jnp.float32)
    for h in range(GROUP):
        here = slice(h * rows, (h + 1) * rows)
        packed = jnp.where(lane == h, peak[here], packed)
        packed = jnp.where(lane == HALF + h, total[here], packed)
    return packed


def image_kernel(owner, q_own, q_pair, keys, values, *rest):
    num_ref, stat_ref = rest[-2:]
    rows = q_own.shape[1]
    scale = 1.0 / DH ** 0.5
    for side, q_ref in enumerate((q_own, q_pair)):
        q = stack_heads(q_ref[0])
        scores = lax.dot_general(
            q, keys[0], (((1,), (1,)), ((), ())), preferred_element_type=jnp.float32
        ) * scale
        peak = jnp.max(scores, axis=-1, keepdims=True)
        expd = jnp.exp(scores - peak)
        total = jnp.sum(expd, axis=-1, keepdims=True)
        num = jnp.dot(expd.astype(jnp.bfloat16), values[0], preferred_element_type=jnp.float32)
        for h in range(GROUP):
            num_ref[0, side, :, h * DH:(h + 1) * DH] = num[h * rows:(h + 1) * rows]
        stat_ref[0, side, 0] = pack_stats(peak, total, rows)


def attend_image(slot, slots, owner, q_own, q_pair, keys, values, carried):
    seqs, rows, columns = q_own.shape
    groups = keys.shape[-1] // DH
    width = columns // groups
    tokens = keys.shape[1]
    q_spec = pl.BlockSpec((1, rows, width), lambda g, own: (own[0], 0, g))
    kv_spec = pl.BlockSpec((1, tokens, DH), lambda g, own: (0, 0, g))
    any_spec = pl.BlockSpec(memory_space=pl.ANY)
    extra = () if carried is None else carried
    pairs = 2 * rows * GROUP * groups * tokens
    return pl.pallas_call(
        image_kernel,
        grid_spec=pltpu.PrefetchScalarGridSpec(
            num_scalar_prefetch=1,
            grid=(groups,),
            in_specs=[q_spec, q_spec, kv_spec, kv_spec] + [any_spec] * len(extra),
            out_specs=[
                pl.BlockSpec((1, 2, rows, width), lambda g, own: (slot, 0, 0, g)),
                pl.BlockSpec((1, 2, 1, rows, LANES), lambda g, own: (slot, 0, g, 0, 0)),
            ],
        ),
        out_shape=[
            jax.ShapeDtypeStruct((slots, 2, rows, columns), jnp.float32),
            jax.ShapeDtypeStruct((slots, 2, groups, rows, LANES), jnp.float32),
        ],
        input_output_aliases={} if carried is None else {5: 0, 6: 1},
        cost_estimate=pl.CostEstimate(
            flops=4 * pairs * DH, bytes_accessed=4 * 2 * rows * columns * 2, transcendentals=pairs
        ),
    )(owner, q_own, q_pair, keys, values, *extra)


def text_kernel(places, q_own, q_pair, keys, values, num_ref, stat_ref, out_ref, out_stat_ref):
    rows = q_own.shape[1]
    count = keys.shape[1]
    scale = 1.0 / DH ** 0.5
    lane = lax.broadcasted_iota(jnp.int32, (1, count), 1)
    key_pos = lane % rows
    for b in range(count // rows):
        inside = (lane >= b * rows) & (lane < (b + 1) * rows)
        key_pos = key_pos + jnp.where(inside, places[2 + b], 0)
    row = lax.broadcasted_iota(jnp.int32, (rows, 1), 0)
    for side, q_ref in enumerate((q_own, q_pair)):
        visible = key_pos <= row + places[side]
        visible = jnp.concatenate([visible.astype(jnp.float32)] * GROUP, axis=0) > 0.5
        q = stack_heads(q_ref[0])
        scores = lax.dot_general(
            q, keys[0], (((1,), (1,)), ((), ())), preferred_element_type=jnp.float32
        ) * scale
        scores = jnp.where(visible, scores, NEG)
        peak = jnp.max(scores, axis=-1, keepdims=True)
        expd = jnp.where(visible, jnp.exp(scores - peak), 0.0)
        total = jnp.sum(expd, axis=-1, keepdims=True)
        num = jnp.dot(expd.astype(jnp.bfloat16), values[0], preferred_element_type=jnp.float32)
        packed = pack_stats(peak, total, rows)
        if side == 0:
            for h in range(GROUP):
                num_ref[0, :, h * DH:(h + 1) * DH] = num[h * rows:(h + 1) * rows]
            stat_ref[0, 0] = packed
        else:
            num = num / jnp.where(total > 0.0, total, 1.0)
            for h in range(GROUP):
                out_ref[0, :, h * DH:(h + 1) * DH] = num[h * rows:(h + 1) * rows].astype(jnp.bfloat16)
            out_stat_ref[0, 0] = packed


def attend_text(places, q_own, q_pair, keys, values):
    seqs, rows, columns = q_own.shape
    groups = keys.shape[-1] // DH
    width = columns // groups
    count = keys.shape[1]
    wide = pl.BlockSpec((1, rows, width), lambda s, g, at: (s, 0, g))
    kv_spec = pl.BlockSpec((1, count, DH), lambda s, g, at: (s, 0, g))
    thin = pl.BlockSpec((1, 1, rows, LANES), lambda s, g, at: (s, g, 0, 0))
    pairs = seqs * 2 * rows * GROUP * groups * count
    stat = jax.ShapeDtypeStruct((seqs, groups, rows, LANES), jnp.float32)
    return pl.pallas_call(
        text_kernel,
        grid_spec=pltpu.PrefetchScalarGridSpec(
            num_scalar_prefetch=1,
            grid=(seqs, groups),
            in_specs=[wide, wide, kv_spec, kv_spec],
            out_specs=[wide, thin, wide, thin],
        ),
        out_shape=[
            jax.ShapeDtypeStruct(q_own.shape, jnp.float32),
            stat,
            jax.ShapeDtypeStruct(q_own.shape, jnp.bfloat16),
            stat,
        ],
        cost_estimate=pl.CostEstimate(
            flops=4 * pairs * DH, bytes_accessed=5 * seqs * rows * columns * 2, transcendentals=pairs
        ),
    )(places, q_own, q_pair, keys, values)


def columns_of(packed, h):
    return packed[:, h:h + 1], packed[:, HALF + h:HALF + h + 1]


def merge_visual(thresholds, base, nums, stats, h, start, more=()):
    rows = nums[0].shape[2]
    row = lax.broadcasted_iota(jnp.int32, (rows, 1), 0) + start
    cut = slice(h * DH, (h + 1) * DH)
    parts = []
    for j, (num, stat) in enumerate(zip(nums, stats)):
        peak, total = columns_of(stat[0, 0, 0], h)
        seen = thresholds[base + j] <= row
        parts.append((jnp.where(seen, peak, NEG), jnp.where(seen, total, 0.0), num[0, 0, :, cut], seen))
    overall = functools.reduce(jnp.maximum, [p[0] for p in parts] + [p[0] for p in more])
    denominator, numerator = 0.0, 0.0
    for peak, total, num, seen in parts:
        weight = jnp.where(seen, jnp.exp(peak - overall), 0.0)
        denominator = denominator + weight * total
        numerator = numerator + weight * num
    for peak, total, out in more:
        weight = jnp.exp(peak - overall) * total
        denominator = denominator + weight
        numerator = numerator + weight * out
    return overall, denominator, numerator


def partial_kernel(per_seq, slots, thresholds, starts, *refs):
    nums, stats = refs[:per_seq], refs[per_seq:2 * per_seq]
    out_ref, stat_ref = refs[2 * per_seq:]
    base = pl.program_id(0) * per_seq
    peaks, totals = [], []
    for h in range(GROUP):
        peak, total, num = merge_visual(thresholds, base, nums, stats, h, starts[1])
        out_ref[0, :, h * DH:(h + 1) * DH] = (num / jnp.where(total > 0.0, total, 1.0)).astype(jnp.bfloat16)
        peaks.append(peak)
        totals.append(total)
    rows = out_ref.shape[1]
    stat_ref[0, 0] = pack_stats(jnp.concatenate(peaks, 0), jnp.concatenate(totals, 0), rows)


def final_kernel(per_seq, slots, thresholds, starts, *refs):
    nums, stats = refs[:per_seq], refs[per_seq:2 * per_seq]
    v_out, v_stat, t_num, t_stat, t_out, t_stat2, gate_ref, out_ref = refs[2 * per_seq:]
    base = pl.program_id(0) * per_seq
    for h in range(GROUP):
        cut = slice(h * DH, (h + 1) * DH)
        peak, total = columns_of(v_stat[0, 0], h)
        other = (peak, total, v_out[0, :, cut].astype(jnp.float32))
        _, v_total, v_sum = merge_visual(thresholds, base, nums, stats, h, starts[0], (other,))
        peak_a, total_a = columns_of(t_stat[0, 0], h)
        peak_b, total_b = columns_of(t_stat2[0, 0], h)
        overall = jnp.maximum(peak_a, peak_b)
        weight_a, weight_b = jnp.exp(peak_a - overall), jnp.exp(peak_b - overall) * total_b
        t_total = weight_a * total_a + weight_b
        t_sum = weight_a * t_num[0, :, cut] + weight_b * t_out[0, :, cut].astype(jnp.float32)
        gate = gate_ref[0, 0][:, h:h + 1]
        mixed = ((1.0 - gate) / t_total) * t_sum + (gate / v_total) * v_sum
        out_ref[0, :, cut] = mixed.astype(jnp.bfloat16)


def merge(kernel, side, per_seq, tables, num, stat, extras, shape, with_stat):
    seqs, rows, columns = shape
    groups = stat.shape[2]
    width = columns // groups

    def num_spec(j):
        return pl.BlockSpec(
            (1, 1, rows, width), lambda s, g, at, th, st: (at[s * per_seq + j], side, 0, g)
        )

    def stat_spec(j):
        return pl.BlockSpec(
            (1, 1, 1, rows, LANES), lambda s, g, at, th, st: (at[s * per_seq + j], side, g, 0, 0)
        )

    wide = pl.BlockSpec((1, rows, width), lambda s, g, at, th, st: (s, 0, g))
    thin = pl.BlockSpec((1, 1, rows, LANES), lambda s, g, at, th, st: (s, g, 0, 0))
    out_specs, out_shape = [wide], [jax.ShapeDtypeStruct(shape, jnp.bfloat16)]
    if with_stat:
        out_specs.append(thin)
        out_shape.append(jax.ShapeDtypeStruct((seqs, groups, rows, LANES), jnp.float32))
    return pl.pallas_call(
        functools.partial(kernel, per_seq),
        grid_spec=pltpu.PrefetchScalarGridSpec(
            num_scalar_prefetch=3,
            grid=(seqs, groups),
            in_specs=[num_spec(j) for j in range(per_seq)]
            + [stat_spec(j) for j in range(per_seq)]
            + [wide if e.ndim == 3 else thin for e in extras],
            out_specs=out_specs,
        ),
        out_shape=out_shape,
        cost_estimate=pl.CostEstimate(
            flops=seqs * rows * columns * 20,
            bytes_accessed=seqs * rows * columns * 24,
            transcendentals=seqs * rows * LANES * 10,
        ),
    )(*tables, *[num] * per_seq, *[stat] * per_seq, *extras)


def on_device(n, heads_split, queries, text_keys, text_values, visual_keys, visual_values,
              gate_weight, text_offsets, image_sequence, image_position):
    seqs, rows, columns = queries.shape
    groups = text_keys.shape[-1] // DH
    here = visual_keys.shape[0]
    me = lax.axis_index("seq")
    members = n // 4
    pair_perm = [(i, i ^ 2) for i in range(n)]
    side_perm = [(i, i ^ 1) for i in range(n)]

    def far_perm(k):
        return [(i, (i // 4 + k) % members * 4 + i % 4) for i in range(n)]

    def send(arrays, perm):
        return tuple(lax.ppermute(a, "seq", perm) for a in arrays)

    q_pair = lax.ppermute(queries, "seq", pair_perm)
    images = [(visual_keys[j:j + 1], visual_values[j:j + 1]) for j in range(here)]
    text_here = (text_keys, text_values)
    sources, texts, pieces = [me], [text_here], [images]
    far_ids = [(me // 4 + members - k) % members * 4 + me % 4 for k in range(1, members)]
    text_far = [send(text_here, far_perm(k)) for k in range(1, members)]
    text_side = send(text_here, side_perm)
    image_far = [[send(image, far_perm(k)) for image in images] for k in range(1, members)]
    image_side = [send(image, side_perm) for image in images]
    text_diag = [send(t, side_perm) for t in text_far]
    image_diag = [[send(image, side_perm) for image in far] for far in image_far]
    sources += [me ^ 1] + far_ids + [f ^ 1 for f in far_ids]
    texts += [text_side] + text_far + text_diag
    pieces += [image_side] + image_far + image_diag

    partial_gate = jnp.dot(
        queries.reshape(seqs * rows, columns).astype(jnp.float32),
        gate_weight,
        precision=lax.Precision.HIGHEST,
    ).reshape(seqs, rows, heads_split, groups * GROUP)
    core = lax.axis_index("kvh")

    def share(k):
        return lax.dynamic_index_in_dim(partial_gate, (core + k) % heads_split, 2, keepdims=False)

    logits = share(0)
    for k in range(1, heads_split):
        logits = logits + lax.ppermute(
            share(k), "kvh", [(c, (c + k) % heads_split) for c in range(heads_split)]
        )
    gate = jax.nn.sigmoid(logits).reshape(seqs, rows, groups, GROUP).transpose(0, 2, 1, 3)
    gate = jnp.pad(gate, ((0, 0), (0, 0), (0, 0), (0, LANES - GROUP)))

    source_ids = jnp.stack(sources)
    starts = jnp.stack([text_offsets[me], text_offsets[me ^ 2]])
    image_ids = (source_ids[:, None] * here + jnp.arange(here, dtype=jnp.int32)).reshape(-1)
    owners = image_sequence[image_ids]
    slots = image_ids.shape[0]
    per_seq = image_sequence.shape[0] // seqs
    mine = owners[None, :] == jnp.arange(seqs, dtype=jnp.int32)[:, None]
    rank = jnp.cumsum(mine.astype(jnp.int32), axis=1) - 1
    pick = mine[:, None, :] & (rank[:, None, :] == jnp.arange(per_seq, dtype=jnp.int32)[None, :, None])
    slot_ids = jnp.arange(slots, dtype=jnp.int32)
    at = jnp.sum(jnp.where(pick, slot_ids, 0), axis=-1).reshape(-1)
    thresholds = jnp.sum(jnp.where(pick, image_position[image_ids], 0), axis=-1)
    thresholds = jnp.where(jnp.any(pick, axis=-1), thresholds, FAR).reshape(-1)
    tables = (at, thresholds, starts)

    all_keys = jnp.concatenate([t[0] for t in texts], axis=1)
    all_values = jnp.concatenate([t[1] for t in texts], axis=1)
    places = jnp.concatenate([starts, text_offsets[source_ids]])
    t_num, t_stat, t_out, t_out_stat = attend_text(places, queries, q_pair, all_keys, all_values)
    t_out, t_out_stat = send((t_out, t_out_stat), pair_perm)

    carried, slot = None, 0
    for group in pieces:
        for keys, values in group:
            carried = attend_image(
                slot, slots, owners[slot:slot + 1], queries, q_pair, keys, values, carried
            )
            slot += 1
    num, stat = carried
    v_out, v_stat = merge(
        partial_kernel, 1, per_seq, tables, num, stat, (), queries.shape, True
    )
    v_out, v_stat = send((v_out, v_stat), pair_perm)
    (mixed,) = merge(
        final_kernel, 0, per_seq, tables, num, stat,
        (v_out, v_stat, t_num, t_stat, t_out, t_out_stat, gate), queries.shape, False,
    )
    return mixed


def solution(mesh):
    return jax.shard_map(
        functools.partial(on_device, mesh.shape["seq"], mesh.shape["kvh"]),
        mesh=mesh,
        in_specs=(
            P("batch", "seq", "kvh"),
            P("batch", "seq", "kvh"),
            P("batch", "seq", "kvh"),
            P(("batch", "seq"), None, "kvh"),
            P(("batch", "seq"), None, "kvh"),
            P("kvh", None),
            P("batch"),
            P("batch"),
            P("batch"),
        ),
        out_specs=P("batch", "seq", "kvh"),
        check_vma=False,
    )
```

```python
import functools
import math

import jax
import jax.numpy as jnp
from jax import lax
from jax.experimental import pallas as pl
from jax.experimental.pallas import tpu as pltpu
from jax.sharding import PartitionSpec as P

DH = 128
GROUP = 7
LANES = 128
HALF = LANES // 2
NEG = -1e30
FLOOR = -1e29
FAR = 1 << 30
SCALE = 1.0 / DH ** 0.5
SCALE2 = SCALE * math.log2(math.e)


def heads_of(ref, lead, g):
    start = pl.multiple_of(g * (GROUP * DH), DH)
    return jnp.concatenate(
        [ref[lead, :, pl.ds(start + h * DH, DH)] for h in range(GROUP)], axis=0
    )


def put_heads(ref, lead, g, stacked):
    rows = stacked.shape[0] // GROUP
    start = pl.multiple_of(g * (GROUP * DH), DH)
    for h in range(GROUP):
        ref[(*lead, slice(None), pl.ds(start + h * DH, DH))] = stacked[h * rows:(h + 1) * rows]


def pack_stats(peak, total, rows):
    lane = lax.broadcasted_iota(jnp.int32, (rows, LANES), 1)
    packed = jnp.zeros((rows, LANES), jnp.float32)
    for h in range(GROUP):
        here = slice(h * rows, (h + 1) * rows)
        packed = jnp.where(lane == h, peak[here], packed)
        packed = jnp.where(lane == HALF + h, total[here], packed)
    return packed


def totals_of(packed):
    return pltpu.roll(packed, HALF, 1)


def softmax_parts(q, keys, values, bias):
    scores = lax.dot_general(
        q, keys, (((1,), (1,)), ((), ())), preferred_element_type=jnp.float32
    )
    if bias is not None:
        rows, count = bias.shape
        scores = (scores.reshape(GROUP, rows, count) + bias[None]).reshape(GROUP * rows, count)
    peak = jnp.maximum(jnp.max(scores, axis=-1, keepdims=True), FLOOR)
    expd = jnp.exp2((scores - peak) * SCALE2)
    total = jnp.sum(expd, axis=-1, keepdims=True)
    num = jnp.dot(expd.astype(jnp.bfloat16), values, preferred_element_type=jnp.float32)
    return peak * SCALE, total, num


def attention_kernel(
    n, seqs, rows, groups, here, per_seq,
    owners, places, at, thresholds,
    queries, text_keys, text_values, visual_keys, visual_values,
    text_ref, visual_ref,
    q_pair, far_tk, far_tv, far_ik, far_iv, num, stat, cat_k, cat_v,
    t_send, t_stat_send, t_recv, t_stat_recv, v_send, v_stat_send, v_recv, v_stat_recv,
    t_own_stat, send_sems, recv_sems,
):
    me = lax.axis_index("seq")
    members = n // 4
    blocks = n // 2
    pair = me // 4 * 4 + (me + 2) % 4
    side = me // 2 * 2 + (me + 1) % 2
    others = [(me // 4 + k) % members * 4 + me % 4 for k in range(1, members)]

    barrier = pltpu.get_barrier_semaphore()
    for peer in (pair, side, *others):
        pl.semaphore_signal(
            barrier, inc=1, device_id={"seq": peer}, device_id_type=pl.DeviceIdType.MESH
        )
    pl.semaphore_wait(barrier, 2 + len(others))

    copies = []

    def send(src, dst, peer):
        copy = pltpu.make_async_remote_copy(
            src_ref=src,
            dst_ref=dst,
            send_sem=send_sems.at[len(copies)],
            recv_sem=recv_sems.at[len(copies)],
            device_id={"seq": peer},
            device_id_type=pl.DeviceIdType.MESH,
        )
        copy.start()
        copies.append(copy)
        return copy

    def slot_of(kind, k=0):
        return {"side": 0, "far": k, "diag": members - 1 + k}[kind]

    q_copy = send(queries, q_pair, pair)
    text_far = []
    for k, peer in enumerate(others, 1):
        s = slot_of("far", k)
        text_far.append((send(text_keys, far_tk.at[s], peer), send(text_values, far_tv.at[s], peer)))
    text_side = (send(text_keys, far_tk.at[0], side), send(text_values, far_tv.at[0], side))
    image_far = {}
    image_side = {}
    for j in range(here):
        for k, peer in enumerate(others, 1):
            s = slot_of("far", k)
            image_far[k, j] = (
                send(visual_keys.at[j], far_ik.at[s, j], peer),
                send(visual_values.at[j], far_iv.at[s, j], peer),
            )
        image_side[j] = (
            send(visual_keys.at[j], far_ik.at[0, j], side),
            send(visual_values.at[j], far_iv.at[0, j], side),
        )

    def attend(keys, values, index, sides):
        owner = owners[index]

        def step(g, carry):
            at_g = pl.ds(pl.multiple_of(g * DH, DH), DH)
            k, v = keys[:, at_g], values[:, at_g]
            for which in sides:
                q = heads_of(queries if which == 0 else q_pair, owner, g)
                peak, total, out = softmax_parts(q, k, v, None)
                put_heads(num, (index, which), g, out)
                stat[index, which, g] = pack_stats(peak, total, rows)
            return carry

        lax.fori_loop(0, groups, step, 0)

    for j in range(here):
        attend(visual_keys.at[j], visual_values.at[j], j, (0,))

    text_diag = []
    for k, pieces in enumerate(text_far, 1):
        for piece in pieces:
            piece.wait_recv()
        s, d = slot_of("far", k), slot_of("diag", k)
        text_diag.append((
            send(far_tk.at[s], far_tk.at[d], side), send(far_tv.at[s], far_tv.at[d], side)
        ))

    q_copy.wait_recv()
    for j in range(here):
        attend(visual_keys.at[j], visual_values.at[j], j, (1,))

    for piece in (*text_side, *[p for pieces in text_diag for p in pieces]):
        piece.wait_recv()
    for b in range(blocks):
        span = pl.ds(b * rows, rows)
        cat_k[:, span, :] = text_keys[...] if b == 0 else far_tk[b - 1]
        cat_v[:, span, :] = text_values[...] if b == 0 else far_tv[b - 1]
    count = blocks * rows
    lane = lax.broadcasted_iota(jnp.int32, (rows, count), 1)
    row = lax.broadcasted_iota(jnp.int32, (rows, count), 0)
    key_pos = lane % rows
    for b in range(blocks):
        inside = (lane >= b * rows) & (lane < (b + 1) * rows)
        key_pos = key_pos + jnp.where(inside, places[2 + b], 0)
    biases = [jnp.where(key_pos <= row + places[which], 0.0, NEG) for which in (0, 1)]

    def text_step(i, carry):
        s, g = i // groups, i % groups
        at_g = pl.ds(pl.multiple_of(g * DH, DH), DH)
        k, v = cat_k[s, :, at_g], cat_v[s, :, at_g]
        peak, total, out = softmax_parts(heads_of(queries, s, g), k, v, biases[0])
        put_heads(text_ref, (s,), g, out)
        t_own_stat[s, g] = pack_stats(peak, total, rows)
        peak, total, out = softmax_parts(heads_of(q_pair, s, g), k, v, biases[1])
        out = out * (1.0 / jnp.where(total > 0.0, total, 1.0))
        put_heads(t_send, (s,), g, out.astype(jnp.bfloat16))
        t_stat_send[s, g] = pack_stats(peak, total, rows)
        return carry

    lax.fori_loop(0, seqs * groups, text_step, 0)
    text_back = (send(t_send, t_recv, pair), send(t_stat_send, t_stat_recv, pair))

    image_diag = {}

    def forward(j):
        for k in range(1, members):
            s, d = slot_of("far", k), slot_of("diag", k)
            pieces = image_far[k, j]
            pieces[0].wait_recv()
            first = send(far_ik.at[s, j], far_ik.at[d, j], side)
            pieces[1].wait_recv()
            image_diag[k, j] = (first, send(far_iv.at[s, j], far_iv.at[d, j], side))

    def attend_far(slot, j):
        attend(far_ik.at[slot, j], far_iv.at[slot, j], (slot + 1) * here + j, (1, 0))

    for j in range(here):
        for piece in image_side[j]:
            piece.wait_recv()
        attend_far(0, j)
    for j in range(here):
        forward(j)
        for k in range(1, members):
            attend_far(slot_of("far", k), j)
        for k in range(1, members):
            for piece in image_diag[k, j]:
                piece.wait_recv()
            attend_far(slot_of("diag", k), j)

    row_pos = lax.broadcasted_iota(jnp.int32, (rows, LANES), 0)

    def visual_weights(s, g, which):
        seen, packed = [], []
        for j in range(per_seq):
            seen.append(thresholds[s * per_seq + j] <= row_pos + places[which])
            packed.append(stat[at[s * per_seq + j], which, g])
        peaks = [jnp.where(a, p, NEG) for a, p in zip(seen, packed)]
        overall = functools.reduce(jnp.maximum, peaks)
        weights = [jnp.where(a, jnp.exp(p - overall), 0.0) for a, p in zip(seen, peaks)]
        total = sum(w * totals_of(p) for w, p in zip(weights, packed))
        return overall, total, weights

    def weighted(s, g, which, h, weights):
        start = pl.multiple_of(g * (GROUP * DH), DH)
        return sum(
            w[:, h:h + 1] * num[at[s * per_seq + j], which, :, pl.ds(start + h * DH, DH)]
            for j, w in enumerate(weights)
        )

    def stat_lanes(overall, total):
        lane_id = lax.broadcasted_iota(jnp.int32, (rows, LANES), 1)
        return jnp.where(lane_id < HALF, overall, pltpu.roll(total, HALF, 1))

    visual_back = []
    for s in range(seqs):
        def pair_step(g, carry, s=s):
            overall, total, weights = visual_weights(s, g, 1)
            inverse = 1.0 / jnp.where(total > 0.0, total, 1.0)
            weights = [w * inverse for w in weights]
            start = pl.multiple_of(g * (GROUP * DH), DH)
            for h in range(GROUP):
                v_send[s, :, pl.ds(start + h * DH, DH)] = weighted(s, g, 1, h, weights).astype(
                    jnp.bfloat16
                )
            v_stat_send[s, g] = stat_lanes(overall, total)
            return carry

        lax.fori_loop(0, groups, pair_step, 0)
        visual_back.append((
            send(v_send.at[s], v_recv.at[s], pair), send(v_stat_send.at[s], v_stat_recv.at[s], pair)
        ))

    for piece in text_back:
        piece.wait_recv()

    def text_merge(i, carry):
        s, g = i // groups, i % groups
        ours, theirs = t_own_stat[s, g], t_stat_recv[s, g]
        overall = jnp.maximum(ours, theirs)
        weight_a = jnp.exp(ours - overall)
        weight_b = jnp.exp(theirs - overall) * totals_of(theirs)
        inverse = 1.0 / (weight_a * totals_of(ours) + weight_b)
        weight_a, weight_b = weight_a * inverse, weight_b * inverse
        start = pl.multiple_of(g * (GROUP * DH), DH)
        for h in range(GROUP):
            cut = pl.ds(start + h * DH, DH)
            text_ref[s, :, cut] = weight_a[:, h:h + 1] * text_ref[s, :, cut] + weight_b[
                :, h:h + 1
            ] * t_recv[s, :, cut].astype(jnp.float32)
        return carry

    lax.fori_loop(0, seqs * groups, text_merge, 0)

    for s in range(seqs):
        for piece in visual_back[s]:
            piece.wait_recv()

        def own_step(g, carry, s=s):
            overall, total, weights = visual_weights(s, g, 0)
            theirs = v_stat_recv[s, g]
            joint = jnp.maximum(overall, theirs)
            weight_a = jnp.exp(overall - joint)
            weight_b = jnp.exp(theirs - joint) * totals_of(theirs)
            inverse = 1.0 / (weight_a * total + weight_b)
            weights = [w * (weight_a * inverse) for w in weights]
            weight_b = weight_b * inverse
            start = pl.multiple_of(g * (GROUP * DH), DH)
            for h in range(GROUP):
                cut = pl.ds(start + h * DH, DH)
                visual_ref[s, :, cut] = weighted(s, g, 0, h, weights) + weight_b[
                    :, h:h + 1
                ] * v_recv[s, :, cut].astype(jnp.float32)
            return carry

        lax.fori_loop(0, groups, own_step, 0)

    for copy in copies:
        copy.wait_send()


def mix_kernel(gate_ref, text_ref, visual_ref, out_ref):
    gate = gate_ref[0]
    for h in range(gate.shape[-1]):
        cut = slice(h * DH, (h + 1) * DH)
        g = gate[:, h:h + 1]
        out_ref[0, :, cut] = ((1.0 - g) * text_ref[0, :, cut] + g * visual_ref[0, :, cut]).astype(
            jnp.bfloat16
        )


def on_device(n, heads_split, queries, text_keys, text_values, visual_keys, visual_values,
              gate_weight, text_offsets, image_sequence, image_position):
    seqs, rows, columns = queries.shape
    groups = text_keys.shape[-1] // DH
    here, tokens, kv_columns = visual_keys.shape
    me = lax.axis_index("seq")
    members, blocks = n // 4, n // 2

    partial_gate = jnp.dot(
        queries.reshape(seqs * rows, columns).astype(jnp.float32),
        gate_weight,
        precision=lax.Precision.HIGHEST,
    ).reshape(seqs, rows, heads_split, groups * GROUP)
    core = lax.axis_index("kvh")

    def share(k):
        return lax.dynamic_index_in_dim(partial_gate, (core + k) % heads_split, 2, keepdims=False)

    logits = share(0)
    for k in range(1, heads_split):
        logits = logits + lax.ppermute(
            share(k), "kvh", [(c, (c + k) % heads_split) for c in range(heads_split)]
        )
    gate = jax.nn.sigmoid(logits)

    far_ids = [(me // 4 + members - k) % members * 4 + me % 4 for k in range(1, members)]
    sources = jnp.stack([me, me ^ 1] + far_ids + [f ^ 1 for f in far_ids])
    image_ids = (sources[:, None] * here + jnp.arange(here, dtype=jnp.int32)).reshape(-1)
    owners = image_sequence[image_ids]
    slots = blocks * here
    per_seq = image_sequence.shape[0] // seqs
    mine = owners[None, :] == jnp.arange(seqs, dtype=jnp.int32)[:, None]
    rank = jnp.cumsum(mine.astype(jnp.int32), axis=1) - 1
    pick = mine[:, None, :] & (rank[:, None, :] == jnp.arange(per_seq, dtype=jnp.int32)[None, :, None])
    at = jnp.sum(jnp.where(pick, jnp.arange(slots, dtype=jnp.int32), 0), axis=-1).reshape(-1)
    thresholds = jnp.sum(jnp.where(pick, image_position[image_ids], 0), axis=-1)
    thresholds = jnp.where(jnp.any(pick, axis=-1), thresholds, FAR).reshape(-1)
    places = text_offsets[jnp.concatenate([jnp.stack([me, me ^ 2]), sources])]

    smem = pl.BlockSpec(memory_space=pltpu.SMEM)
    vmem = pl.BlockSpec(memory_space=pltpu.VMEM)
    bf16, f32 = jnp.bfloat16, jnp.float32
    count = 1 + 4 * (members - 1) + 2 + here * (4 * (members - 1) + 2) + 2 + 2 * seqs
    stats = (seqs, groups, rows, LANES)
    pairs = 2 * rows * GROUP * groups * (slots * tokens + seqs * blocks * rows)
    text, visual = pl.pallas_call(
        functools.partial(attention_kernel, n, seqs, rows, groups, here, per_seq),
        in_specs=[smem] * 4 + [vmem] * 5,
        out_specs=[vmem, vmem],
        out_shape=[jax.ShapeDtypeStruct(queries.shape, f32)] * 2,
        scratch_shapes=[
            pltpu.VMEM(queries.shape, bf16),
            pltpu.VMEM((blocks - 1, *text_keys.shape), bf16),
            pltpu.VMEM((blocks - 1, *text_keys.shape), bf16),
            pltpu.VMEM((blocks - 1, *visual_keys.shape), bf16),
            pltpu.VMEM((blocks - 1, *visual_keys.shape), bf16),
            pltpu.VMEM((slots, 2, rows, columns), f32),
            pltpu.VMEM((slots, 2, groups, rows, LANES), f32),
            pltpu.VMEM((seqs, blocks * rows, kv_columns), bf16),
            pltpu.VMEM((seqs, blocks * rows, kv_columns), bf16),
            pltpu.VMEM(queries.shape, bf16),
            pltpu.VMEM(stats, f32),
            pltpu.VMEM(queries.shape, bf16),
            pltpu.VMEM(stats, f32),
            pltpu.VMEM(queries.shape, bf16),
            pltpu.VMEM(stats, f32),
            pltpu.VMEM(queries.shape, bf16),
            pltpu.VMEM(stats, f32),
            pltpu.VMEM(stats, f32),
            pltpu.SemaphoreType.DMA((count,)),
            pltpu.SemaphoreType.DMA((count,)),
        ],
        compiler_params=pltpu.CompilerParams(
            collective_id=0, has_side_effects=True, vmem_limit_bytes=60 << 20
        ),
        cost_estimate=pl.CostEstimate(
            flops=4 * pairs * DH, bytes_accessed=16 << 20, transcendentals=pairs
        ),
    )(owners, places, at, thresholds, queries, text_keys, text_values, visual_keys, visual_values)

    wide = pl.BlockSpec((1, rows, columns), lambda s: (s, 0, 0))
    return pl.pallas_call(
        mix_kernel,
        grid=(seqs,),
        in_specs=[pl.BlockSpec((1, rows, groups * GROUP), lambda s: (s, 0, 0)), wide, wide],
        out_specs=wide,
        out_shape=jax.ShapeDtypeStruct(queries.shape, bf16),
    )(gate, text, visual)


def solution(mesh):
    return jax.shard_map(
        functools.partial(on_device, mesh.shape["seq"], mesh.shape["kvh"]),
        mesh=mesh,
        in_specs=(
            P("batch", "seq", "kvh"),
            P("batch", "seq", "kvh"),
            P("batch", "seq", "kvh"),
            P(("batch", "seq"), None, "kvh"),
            P(("batch", "seq"), None, "kvh"),
            P("kvh", None),
            P("batch"),
            P("batch"),
            P("batch"),
        ),
        out_specs=P("batch", "seq", "kvh"),
        check_vma=False,
    )
```

```python
import functools
import math

import jax
import jax.numpy as jnp
from jax import lax
from jax.experimental import pallas as pl
from jax.experimental.pallas import tpu as pltpu
from jax.sharding import PartitionSpec as P

DH = 128
GROUP = 7
LANES = 128
HALF = LANES // 2
NEG = -1e30
FLOOR = -1e29
FAR = 1 << 30
SCALE = 1.0 / DH ** 0.5
SCALE2 = SCALE * math.log2(math.e)


def heads_of(ref, lead, g):
    start = pl.multiple_of(g * (GROUP * DH), DH)
    return jnp.concatenate(
        [ref[lead, :, pl.ds(start + h * DH, DH)] for h in range(GROUP)], axis=0
    )


def put_heads(ref, lead, g, stacked):
    rows = stacked.shape[0] // GROUP
    start = pl.multiple_of(g * (GROUP * DH), DH)
    for h in range(GROUP):
        ref[(*lead, slice(None), pl.ds(start + h * DH, DH))] = stacked[h * rows:(h + 1) * rows]


def pack_stats(peak, total, rows):
    lane = lax.broadcasted_iota(jnp.int32, (rows, LANES), 1)
    packed = jnp.zeros((rows, LANES), jnp.float32)
    for h in range(GROUP):
        here = slice(h * rows, (h + 1) * rows)
        packed = jnp.where(lane == h, peak[here], packed)
        packed = jnp.where(lane == HALF + h, total[here], packed)
    return packed


def totals_of(packed):
    return pltpu.roll(packed, HALF, 1)


def softmax_parts(q, keys, values, bias):
    scores = lax.dot_general(
        q, keys, (((1,), (1,)), ((), ())), preferred_element_type=jnp.float32
    )
    if bias is not None:
        rows, count = bias.shape
        scores = (scores.reshape(GROUP, rows, count) + bias[None]).reshape(GROUP * rows, count)
    peak = jnp.maximum(jnp.max(scores, axis=-1, keepdims=True), FLOOR)
    expd = jnp.exp2((scores - peak) * SCALE2)
    total = jnp.sum(expd, axis=-1, keepdims=True)
    num = jnp.dot(expd.astype(jnp.bfloat16), values, preferred_element_type=jnp.float32)
    return peak * SCALE, total, num


def attention_kernel(
    n, heads_split, seqs, rows, groups, here, per_seq,
    offsets, image_sequence, image_position,
    queries, text_keys, text_values, visual_keys, visual_values, gate_weight,
    out_ref,
    q_pair, far_tk, far_tv, far_ik, far_iv, num, stat, cat_k, cat_v,
    t_send, t_stat_send, t_recv, t_stat_recv, v_send, v_stat_send, v_recv, v_stat_recv,
    t_own, t_own_stat, gate_own, gate_recv, gate_buf, send_sems, recv_sems,
):
    me = lax.axis_index("seq")
    core = lax.axis_index("kvh")
    members = n // 4
    blocks = n // 2
    pair = me // 4 * 4 + (me + 2) % 4
    side = me // 2 * 2 + (me + 1) % 2
    others = [(me // 4 + k) % members * 4 + me % 4 for k in range(1, members)]
    twins = [(core + k) % heads_split for k in range(1, heads_split)]

    far_ids = [(me // 4 + members - k) % members * 4 + me % 4 for k in range(1, members)]
    sources = [me, side] + far_ids + [f // 2 * 2 + (f + 1) % 2 for f in far_ids]
    places = [offsets[i] for i in (me, pair, *sources)]
    image_ids = [source * here + j for source in sources for j in range(here)]
    owners = [image_sequence[i] for i in image_ids]
    positions = [image_position[i] for i in image_ids]
    at, thresholds = [], []
    for s in range(seqs):
        slot_here = [jnp.int32(0)] * per_seq
        threshold_here = [jnp.int32(FAR)] * per_seq
        found = jnp.int32(0)
        for slot, (owner, position) in enumerate(zip(owners, positions)):
            hit = owner == s
            for j in range(per_seq):
                take = hit & (found == j)
                slot_here[j] = jnp.where(take, slot, slot_here[j])
                threshold_here[j] = jnp.where(take, position, threshold_here[j])
            found = found + jnp.where(hit, 1, 0)
        at += slot_here
        thresholds += threshold_here

    barrier = pltpu.get_barrier_semaphore()
    for peer in (pair, side, *others):
        pl.semaphore_signal(
            barrier, inc=1, device_id={"seq": peer}, device_id_type=pl.DeviceIdType.MESH
        )
    for twin in twins:
        pl.semaphore_signal(
            barrier, inc=1, device_id={"kvh": twin}, device_id_type=pl.DeviceIdType.MESH
        )
    pl.semaphore_wait(barrier, 2 + len(others) + len(twins))

    copies = []

    def send(src, dst, peer, axis="seq"):
        copy = pltpu.make_async_remote_copy(
            src_ref=src,
            dst_ref=dst,
            send_sem=send_sems.at[len(copies)],
            recv_sem=recv_sems.at[len(copies)],
            device_id={axis: peer},
            device_id_type=pl.DeviceIdType.MESH,
        )
        copy.start()
        copies.append(copy)
        return copy

    def slot_of(kind, k=0):
        return {"side": 0, "far": k, "diag": members - 1 + k}[kind]

    q_copy = send(queries, q_pair, pair)
    text_far = []
    for k, peer in enumerate(others, 1):
        s = slot_of("far", k)
        text_far.append((send(text_keys, far_tk.at[s], peer), send(text_values, far_tv.at[s], peer)))
    text_side = (send(text_keys, far_tk.at[0], side), send(text_values, far_tv.at[0], side))
    image_far = {}
    image_side = {}
    for j in range(here):
        for k, peer in enumerate(others, 1):
            s = slot_of("far", k)
            image_far[k, j] = (
                send(visual_keys.at[j], far_ik.at[s, j], peer),
                send(visual_values.at[j], far_iv.at[s, j], peer),
            )
        image_side[j] = (
            send(visual_keys.at[j], far_ik.at[0, j], side),
            send(visual_values.at[j], far_iv.at[0, j], side),
        )

    def attend(keys, values, index, sides):
        owner = owners[index]

        def step(g, carry):
            at_g = pl.ds(pl.multiple_of(g * DH, DH), DH)
            k, v = keys[:, at_g], values[:, at_g]
            for which in sides:
                q = heads_of(queries if which == 0 else q_pair, owner, g)
                peak, total, out = softmax_parts(q, k, v, None)
                put_heads(num, (index, which), g, out)
                stat[index, which, g] = pack_stats(peak, total, rows)
            return carry

        lax.fori_loop(0, groups, step, 0)

    rest = gate_weight[...]
    q_all = queries[...].reshape(seqs * rows, queries.shape[-1])
    logits = 0.0
    for _ in range(3):
        term = rest.astype(jnp.bfloat16)
        rest = rest - term.astype(jnp.float32)
        logits = logits + jnp.dot(q_all, term, preferred_element_type=jnp.float32)
    gate_own[...] = logits.reshape(gate_own.shape)
    t_stat_send[...] = jnp.zeros_like(t_stat_send)
    v_stat_send[...] = jnp.zeros_like(v_stat_send)

    for j in range(here):
        attend(visual_keys.at[j], visual_values.at[j], j, (0,))
    gates = [send(gate_own, gate_recv.at[k], twin, "kvh") for k, twin in enumerate(twins)]

    text_diag = []
    for k, pieces in enumerate(text_far, 1):
        for piece in pieces:
            piece.wait_recv()
        s, d = slot_of("far", k), slot_of("diag", k)
        text_diag.append((
            send(far_tk.at[s], far_tk.at[d], side), send(far_tv.at[s], far_tv.at[d], side)
        ))

    q_copy.wait_recv()
    for j in range(here):
        attend(visual_keys.at[j], visual_values.at[j], j, (1,))

    for piece in (*text_side, *[p for pieces in text_diag for p in pieces]):
        piece.wait_recv()
    for b in range(blocks):
        span = pl.ds(b * rows, rows)
        cat_k[:, span, :] = text_keys[...] if b == 0 else far_tk[b - 1]
        cat_v[:, span, :] = text_values[...] if b == 0 else far_tv[b - 1]
    count = blocks * rows
    lane = lax.broadcasted_iota(jnp.int32, (rows, count), 1)
    row = lax.broadcasted_iota(jnp.int32, (rows, count), 0)
    key_pos = lane % rows
    for b in range(blocks):
        inside = (lane >= b * rows) & (lane < (b + 1) * rows)
        key_pos = key_pos + jnp.where(inside, places[2 + b], 0)
    biases = [jnp.where(key_pos <= row + places[which], 0.0, NEG) for which in (0, 1)]

    def text_step(i, carry):
        s, g = i // groups, i % groups
        at_g = pl.ds(pl.multiple_of(g * DH, DH), DH)
        k, v = cat_k[s, :, at_g], cat_v[s, :, at_g]
        peak, total, out = softmax_parts(heads_of(queries, s, g), k, v, biases[0])
        put_heads(t_own, (s,), g, out)
        t_own_stat[s, g] = pack_stats(peak, total, rows)
        peak, total, out = softmax_parts(heads_of(q_pair, s, g), k, v, biases[1])
        out = out * (1.0 / jnp.where(total > 0.0, total, 1.0))
        put_heads(t_send, (s,), g, out.astype(jnp.bfloat16))
        t_stat_send[s] = t_stat_send[s] + pltpu.roll(pack_stats(peak, total, rows), g * 8, 1)
        return carry

    lax.fori_loop(0, seqs * groups, text_step, 0)
    text_back = (send(t_send, t_recv, pair), send(t_stat_send, t_stat_recv, pair))

    image_diag = {}

    def forward(j):
        for k in range(1, members):
            s, d = slot_of("far", k), slot_of("diag", k)
            pieces = image_far[k, j]
            pieces[0].wait_recv()
            first = send(far_ik.at[s, j], far_ik.at[d, j], side)
            pieces[1].wait_recv()
            image_diag[k, j] = (first, send(far_iv.at[s, j], far_iv.at[d, j], side))

    def attend_far(slot, j, sides=(1, 0)):
        attend(far_ik.at[slot, j], far_iv.at[slot, j], (slot + 1) * here + j, sides)

    for j in range(here):
        for piece in image_side[j]:
            piece.wait_recv()
        attend_far(0, j)
    for j in range(here):
        forward(j)
        for k in range(1, members):
            attend_far(slot_of("far", k), j)
        for k in range(1, members):
            for piece in image_diag[k, j]:
                piece.wait_recv()
            last = j == here - 1 and k == members - 1
            attend_far(slot_of("diag", k), j, (1,) if last else (1, 0))

    row_pos = lax.broadcasted_iota(jnp.int32, (rows, LANES), 0)

    def visual_weights(s, g, which):
        seen, packed = [], []
        for j in range(per_seq):
            seen.append(thresholds[s * per_seq + j] <= row_pos + places[which])
            packed.append(stat[at[s * per_seq + j], which, g])
        peaks = [jnp.where(a, p, NEG) for a, p in zip(seen, packed)]
        overall = functools.reduce(jnp.maximum, peaks)
        weights = [jnp.where(a, jnp.exp(p - overall), 0.0) for a, p in zip(seen, peaks)]
        total = sum(w * totals_of(p) for w, p in zip(weights, packed))
        return overall, total, weights

    def weighted(s, g, which, h, weights):
        start = pl.multiple_of(g * (GROUP * DH), DH)
        return sum(
            w[:, h:h + 1] * num[at[s * per_seq + j], which, :, pl.ds(start + h * DH, DH)]
            for j, w in enumerate(weights)
        )

    def stat_lanes(overall, total):
        lane_id = lax.broadcasted_iota(jnp.int32, (rows, LANES), 1)
        packed = jnp.where(lane_id < HALF, overall, pltpu.roll(total, HALF, 1))
        return jnp.where(lane_id % HALF < GROUP, packed, 0.0)

    visual_back = []
    for s in range(seqs):
        def pair_step(g, carry, s=s):
            overall, total, weights = visual_weights(s, g, 1)
            inverse = 1.0 / jnp.where(total > 0.0, total, 1.0)
            weights = [w * inverse for w in weights]
            start = pl.multiple_of(g * (GROUP * DH), DH)
            for h in range(GROUP):
                v_send[s, :, pl.ds(start + h * DH, DH)] = weighted(s, g, 1, h, weights).astype(
                    jnp.bfloat16
                )
            v_stat_send[s] = v_stat_send[s] + pltpu.roll(stat_lanes(overall, total), g * 8, 1)
            return carry

        lax.fori_loop(0, groups, pair_step, 0)
        visual_back.append((
            send(v_send.at[s], v_recv.at[s], pair), send(v_stat_send.at[s], v_stat_recv.at[s], pair)
        ))

    attend_far(slot_of("diag", members - 1), here - 1, (0,))

    for piece in gates:
        piece.wait_recv()
    for s in range(seqs):
        logits = gate_own[s]
        for k in range(len(twins)):
            logits = logits + gate_recv[k, s]
        heads = groups * GROUP
        mine = logits[:, :heads]
        for c in range(1, heads_split):
            mine = jnp.where(core == c, logits[:, c * heads:(c + 1) * heads], mine)
        mine = jax.nn.sigmoid(mine)
        for g in range(groups):
            gate_buf[s, g, :, :GROUP] = mine[:, g * GROUP:(g + 1) * GROUP]

    for piece in text_back:
        piece.wait_recv()

    def unpacked(packed, g):
        return pltpu.roll(packed, LANES - g * 8, 1)

    def text_merge(i, carry):
        s, g = i // groups, i % groups
        ours, theirs = t_own_stat[s, g], unpacked(t_stat_recv[s], g)
        overall = jnp.maximum(ours, theirs)
        weight_a = jnp.exp(ours - overall)
        weight_b = jnp.exp(theirs - overall) * totals_of(theirs)
        inverse = 1.0 / (weight_a * totals_of(ours) + weight_b)
        weight_a, weight_b = weight_a * inverse, weight_b * inverse
        start = pl.multiple_of(g * (GROUP * DH), DH)
        for h in range(GROUP):
            cut = pl.ds(start + h * DH, DH)
            t_own[s, :, cut] = weight_a[:, h:h + 1] * t_own[s, :, cut] + weight_b[
                :, h:h + 1
            ] * t_recv[s, :, cut].astype(jnp.float32)
        return carry

    lax.fori_loop(0, seqs * groups, text_merge, 0)

    for s in range(seqs):
        for piece in visual_back[s]:
            piece.wait_recv()

        def own_step(g, carry, s=s):
            overall, total, weights = visual_weights(s, g, 0)
            theirs = unpacked(v_stat_recv[s], g)
            joint = jnp.maximum(overall, theirs)
            weight_a = jnp.exp(overall - joint)
            weight_b = jnp.exp(theirs - joint) * totals_of(theirs)
            inverse = 1.0 / (weight_a * total + weight_b)
            weights = [w * (weight_a * inverse) for w in weights]
            weight_b = weight_b * inverse
            start = pl.multiple_of(g * (GROUP * DH), DH)
            for h in range(GROUP):
                cut = pl.ds(start + h * DH, DH)
                visual = weighted(s, g, 0, h, weights) + weight_b[:, h:h + 1] * v_recv[
                    s, :, cut
                ].astype(jnp.float32)
                gate = gate_buf[s, g, :, h:h + 1]
                out_ref[s, :, cut] = ((1.0 - gate) * t_own[s, :, cut] + gate * visual).astype(
                    jnp.bfloat16
                )
            return carry

        lax.fori_loop(0, groups, own_step, 0)

    for copy in copies:
        copy.wait_send()


def on_device(n, heads_split, queries, text_keys, text_values, visual_keys, visual_values,
              gate_weight, text_offsets, image_sequence, image_position):
    seqs, rows, columns = queries.shape
    groups = text_keys.shape[-1] // DH
    here, tokens, kv_columns = visual_keys.shape
    members, blocks = n // 4, n // 2
    slots = blocks * here
    per_seq = image_sequence.shape[0] // seqs
    smem = pl.BlockSpec(memory_space=pltpu.SMEM)
    vmem = pl.BlockSpec(memory_space=pltpu.VMEM)
    bf16, f32 = jnp.bfloat16, jnp.float32
    count = 1 + 4 * (members - 1) + 2 + here * (4 * (members - 1) + 2) + 2 + 2 * seqs + heads_split - 1
    stats = (seqs, groups, rows, LANES)
    sent_stats = (seqs, rows, LANES)
    gate_shape = (seqs, rows, gate_weight.shape[-1])
    pairs = 2 * rows * GROUP * groups * (slots * tokens + seqs * blocks * rows)
    return pl.pallas_call(
        functools.partial(attention_kernel, n, heads_split, seqs, rows, groups, here, per_seq),
        in_specs=[smem] * 3 + [vmem] * 6,
        out_specs=vmem,
        out_shape=jax.ShapeDtypeStruct(queries.shape, bf16),
        scratch_shapes=[
            pltpu.VMEM(queries.shape, bf16),
            pltpu.VMEM((blocks - 1, *text_keys.shape), bf16),
            pltpu.VMEM((blocks - 1, *text_keys.shape), bf16),
            pltpu.VMEM((blocks - 1, *visual_keys.shape), bf16),
            pltpu.VMEM((blocks - 1, *visual_keys.shape), bf16),
            pltpu.VMEM((slots, 2, rows, columns), f32),
            pltpu.VMEM((slots, 2, groups, rows, LANES), f32),
            pltpu.VMEM((seqs, blocks * rows, kv_columns), bf16),
            pltpu.VMEM((seqs, blocks * rows, kv_columns), bf16),
            pltpu.VMEM(queries.shape, bf16),
            pltpu.VMEM(sent_stats, f32),
            pltpu.VMEM(queries.shape, bf16),
            pltpu.VMEM(sent_stats, f32),
            pltpu.VMEM(queries.shape, bf16),
            pltpu.VMEM(sent_stats, f32),
            pltpu.VMEM(queries.shape, bf16),
            pltpu.VMEM(sent_stats, f32),
            pltpu.VMEM(queries.shape, f32),
            pltpu.VMEM(stats, f32),
            pltpu.VMEM(gate_shape, f32),
            pltpu.VMEM((heads_split - 1, *gate_shape), f32),
            pltpu.VMEM(stats, f32),
            pltpu.SemaphoreType.DMA((count,)),
            pltpu.SemaphoreType.DMA((count,)),
        ],
        compiler_params=pltpu.CompilerParams(
            collective_id=0, has_side_effects=True, vmem_limit_bytes=60 << 20
        ),
        cost_estimate=pl.CostEstimate(
            flops=4 * pairs * DH, bytes_accessed=16 << 20, transcendentals=pairs
        ),
    )(
        text_offsets, image_sequence, image_position,
        queries, text_keys, text_values, visual_keys, visual_values, gate_weight,
    )


def solution(mesh):
    return jax.shard_map(
        functools.partial(on_device, mesh.shape["seq"], mesh.shape["kvh"]),
        mesh=mesh,
        in_specs=(
            P("batch", "seq", "kvh"),
            P("batch", "seq", "kvh"),
            P("batch", "seq", "kvh"),
            P(("batch", "seq"), None, "kvh"),
            P(("batch", "seq"), None, "kvh"),
            P("kvh", None),
            P("batch"),
            P("batch"),
            P("batch"),
        ),
        out_specs=P("batch", "seq", "kvh"),
        check_vma=False,
    )
```

```python
import functools
import math

import jax
import jax.numpy as jnp
from jax import lax
from jax.experimental import pallas as pl
from jax.experimental.pallas import tpu as pltpu
from jax.sharding import PartitionSpec as P

DH = 128
GROUP = 7
LANES = 128
HALF = LANES // 2
CHUNKS = 4
TILE = 16
NEG = -1e30
FLOOR = -1e29
FAR = 1 << 30
SCALE = 1.0 / DH ** 0.5
SCALE2 = SCALE * math.log2(math.e)


def chunks_of(tokens):
    size = -(-tokens // (CHUNKS * TILE)) * TILE
    return [pl.ds(a, min(size, tokens - a)) for a in range(0, tokens, size)]


def heads_of(ref, lead, g):
    start = pl.multiple_of(g * (GROUP * DH), DH)
    return jnp.concatenate(
        [ref[lead, :, pl.ds(start + h * DH, DH)] for h in range(GROUP)], axis=0
    )


def put_heads(ref, lead, g, stacked):
    rows = stacked.shape[0] // GROUP
    start = pl.multiple_of(g * (GROUP * DH), DH)
    for h in range(GROUP):
        ref[(*lead, slice(None), pl.ds(start + h * DH, DH))] = stacked[h * rows:(h + 1) * rows]


def pack_stats(peak, total, rows):
    lane = lax.broadcasted_iota(jnp.int32, (rows, LANES), 1)
    packed = jnp.zeros((rows, LANES), jnp.float32)
    for h in range(GROUP):
        here = slice(h * rows, (h + 1) * rows)
        packed = jnp.where(lane == h, peak[here], packed)
        packed = jnp.where(lane == HALF + h, total[here], packed)
    return packed


def totals_of(packed):
    return pltpu.roll(packed, HALF, 1)


def softmax_parts(q, keys, values, bias):
    scores = lax.dot_general(
        q, keys, (((1,), (1,)), ((), ())), preferred_element_type=jnp.float32
    )
    if bias is not None:
        rows, count = bias.shape
        scores = (scores.reshape(GROUP, rows, count) + bias[None]).reshape(GROUP * rows, count)
    peak = jnp.maximum(jnp.max(scores, axis=-1, keepdims=True), FLOOR)
    expd = jnp.exp2((scores - peak) * SCALE2)
    total = jnp.sum(expd, axis=-1, keepdims=True)
    num = jnp.dot(expd.astype(jnp.bfloat16), values, preferred_element_type=jnp.float32)
    return peak * SCALE, total, num


def attention_kernel(
    n, heads_split, seqs, rows, groups, here, per_seq,
    offsets, image_sequence, image_position,
    queries, text_keys, text_values, visual_keys, visual_values, gate_weight,
    out_ref,
    q_pair, far_tk, far_tv, far_ik, far_iv, num, stat, cat_k, cat_v,
    t_send, t_stat_send, t_recv, t_stat_recv, v_send, v_stat_send, v_recv, v_stat_recv,
    t_own, t_own_stat, gate_own, gate_recv, gate_buf, send_sems, recv_sems,
):
    me = lax.axis_index("seq")
    core = lax.axis_index("kvh")
    members = n // 4
    blocks = n // 2
    pair = me // 4 * 4 + (me + 2) % 4
    side = me // 2 * 2 + (me + 1) % 2
    others = [(me // 4 + k) % members * 4 + me % 4 for k in range(1, members)]
    twins = [(core + k) % heads_split for k in range(1, heads_split)]

    far_ids = [(me // 4 + members - k) % members * 4 + me % 4 for k in range(1, members)]
    sources = [me, side] + far_ids + [f // 2 * 2 + (f + 1) % 2 for f in far_ids]
    places = [offsets[i] for i in (me, pair, *sources)]
    image_ids = [source * here + j for source in sources for j in range(here)]
    owners = [image_sequence[i] for i in image_ids]
    positions = [image_position[i] for i in image_ids]
    at, thresholds = [], []
    for s in range(seqs):
        slot_here = [jnp.int32(0)] * per_seq
        threshold_here = [jnp.int32(FAR)] * per_seq
        found = jnp.int32(0)
        for slot, (owner, position) in enumerate(zip(owners, positions)):
            hit = owner == s
            for j in range(per_seq):
                take = hit & (found == j)
                slot_here[j] = jnp.where(take, slot, slot_here[j])
                threshold_here[j] = jnp.where(take, position, threshold_here[j])
            found = found + jnp.where(hit, 1, 0)
        at += slot_here
        thresholds += threshold_here

    barrier = pltpu.get_barrier_semaphore()
    for peer in (pair, side, *others):
        pl.semaphore_signal(
            barrier, inc=1, device_id={"seq": peer}, device_id_type=pl.DeviceIdType.MESH
        )
    for twin in twins:
        pl.semaphore_signal(
            barrier, inc=1, device_id={"kvh": twin}, device_id_type=pl.DeviceIdType.MESH
        )
    pl.semaphore_wait(barrier, 2 + len(others) + len(twins))

    copies = []
    chunks = chunks_of(visual_values.shape[1])

    def send(src, dst, peer, axis="seq"):
        copy = pltpu.make_async_remote_copy(
            src_ref=src,
            dst_ref=dst,
            send_sem=send_sems.at[len(copies)],
            recv_sem=recv_sems.at[len(copies)],
            device_id={axis: peer},
            device_id_type=pl.DeviceIdType.MESH,
        )
        copy.start()
        copies.append(copy)
        return copy

    def slot_of(kind, k=0):
        return {"side": 0, "far": k, "diag": members - 1 + k}[kind]

    q_copy = send(queries, q_pair, pair)
    text_far = []
    for k, peer in enumerate(others, 1):
        s = slot_of("far", k)
        text_far.append((send(text_keys, far_tk.at[s], peer), send(text_values, far_tv.at[s], peer)))
    text_side = (send(text_keys, far_tk.at[0], side), send(text_values, far_tv.at[0], side))
    image_far = {}
    image_side = {}
    for j in range(here):
        for k, peer in enumerate(others, 1):
            s = slot_of("far", k)
            image_far[k, j] = [send(visual_keys.at[j], far_ik.at[s, j], peer)] + [
                send(visual_values.at[j, cut], far_iv.at[s, j, cut], peer) for cut in chunks
            ]
        image_side[j] = (
            send(visual_keys.at[j], far_ik.at[0, j], side),
            send(visual_values.at[j], far_iv.at[0, j], side),
        )

    def attend(keys, values, index, sides):
        owner = owners[index]

        def step(g, carry):
            at_g = pl.ds(pl.multiple_of(g * DH, DH), DH)
            k, v = keys[:, at_g], values[:, at_g]
            for which in sides:
                q = heads_of(queries if which == 0 else q_pair, owner, g)
                peak, total, out = softmax_parts(q, k, v, None)
                put_heads(num, (index, which), g, out)
                stat[index, which, g] = pack_stats(peak, total, rows)
            return carry

        lax.fori_loop(0, groups, step, 0)

    rest = gate_weight[...]
    q_all = queries[...].reshape(seqs * rows, queries.shape[-1])
    logits = 0.0
    for _ in range(3):
        term = rest.astype(jnp.bfloat16)
        rest = rest - term.astype(jnp.float32)
        logits = logits + lax.dot_general(
            q_all, term, (((1,), (1,)), ((), ())), preferred_element_type=jnp.float32
        )
    gate_own[...] = logits.reshape(gate_own.shape)
    t_stat_send[...] = jnp.zeros_like(t_stat_send)
    v_stat_send[...] = jnp.zeros_like(v_stat_send)

    for j in range(here):
        attend(visual_keys.at[j], visual_values.at[j], j, (0,))
    gates = [send(gate_own, gate_recv.at[k], twin, "kvh") for k, twin in enumerate(twins)]

    text_diag = []
    for k, pieces in enumerate(text_far, 1):
        for piece in pieces:
            piece.wait_recv()
        s, d = slot_of("far", k), slot_of("diag", k)
        text_diag.append((
            send(far_tk.at[s], far_tk.at[d], side), send(far_tv.at[s], far_tv.at[d], side)
        ))

    q_copy.wait_recv()
    for j in range(here):
        attend(visual_keys.at[j], visual_values.at[j], j, (1,))

    for piece in (*text_side, *[p for pieces in text_diag for p in pieces]):
        piece.wait_recv()
    for b in range(blocks):
        span = pl.ds(b * rows, rows)
        cat_k[:, span, :] = text_keys[...] if b == 0 else far_tk[b - 1]
        cat_v[:, span, :] = text_values[...] if b == 0 else far_tv[b - 1]
    count = blocks * rows
    lane = lax.broadcasted_iota(jnp.int32, (rows, count), 1)
    row = lax.broadcasted_iota(jnp.int32, (rows, count), 0)
    key_pos = lane % rows
    for b in range(blocks):
        inside = (lane >= b * rows) & (lane < (b + 1) * rows)
        key_pos = key_pos + jnp.where(inside, places[2 + b], 0)
    biases = [jnp.where(key_pos <= row + places[which], 0.0, NEG) for which in (0, 1)]

    def text_step(i, carry):
        s, g = i // groups, i % groups
        at_g = pl.ds(pl.multiple_of(g * DH, DH), DH)
        k, v = cat_k[s, :, at_g], cat_v[s, :, at_g]
        peak, total, out = softmax_parts(heads_of(queries, s, g), k, v, biases[0])
        put_heads(t_own, (s,), g, out)
        t_own_stat[s, g] = pack_stats(peak, total, rows)
        peak, total, out = softmax_parts(heads_of(q_pair, s, g), k, v, biases[1])
        out = out * (1.0 / jnp.where(total > 0.0, total, 1.0))
        put_heads(t_send, (s,), g, out.astype(jnp.bfloat16))
        t_stat_send[s] = t_stat_send[s] + pltpu.roll(pack_stats(peak, total, rows), g * 8, 1)
        return carry

    lax.fori_loop(0, seqs * groups, text_step, 0)
    text_back = (send(t_send, t_recv, pair), send(t_stat_send, t_stat_recv, pair))

    image_diag = {}

    def forward(j):
        for k in range(1, members):
            s, d = slot_of("far", k), slot_of("diag", k)
            pieces = image_far[k, j]
            pieces[0].wait_recv()
            image_diag[k, j] = [send(far_ik.at[s, j], far_ik.at[d, j], side)]
            for cut, piece in zip(chunks, pieces[1:]):
                piece.wait_recv()
                image_diag[k, j].append(send(far_iv.at[s, j, cut], far_iv.at[d, j, cut], side))

    def attend_far(slot, j, sides=(1, 0)):
        attend(far_ik.at[slot, j], far_iv.at[slot, j], (slot + 1) * here + j, sides)

    for j in range(here):
        for piece in image_side[j]:
            piece.wait_recv()
        attend_far(0, j)
    for j in range(here):
        forward(j)
        for k in range(1, members):
            attend_far(slot_of("far", k), j)
        for k in range(1, members):
            for piece in image_diag[k, j]:
                piece.wait_recv()
            last = j == here - 1 and k == members - 1
            attend_far(slot_of("diag", k), j, (1,) if last else (1, 0))

    row_pos = lax.broadcasted_iota(jnp.int32, (rows, LANES), 0)

    def visual_weights(s, g, which):
        seen, packed = [], []
        for j in range(per_seq):
            seen.append(thresholds[s * per_seq + j] <= row_pos + places[which])
            packed.append(stat[at[s * per_seq + j], which, g])
        peaks = [jnp.where(a, p, NEG) for a, p in zip(seen, packed)]
        overall = functools.reduce(jnp.maximum, peaks)
        weights = [jnp.where(a, jnp.exp(p - overall), 0.0) for a, p in zip(seen, peaks)]
        total = sum(w * totals_of(p) for w, p in zip(weights, packed))
        return overall, total, weights

    def weighted(s, g, which, h, weights):
        start = pl.multiple_of(g * (GROUP * DH), DH)
        return sum(
            w[:, h:h + 1] * num[at[s * per_seq + j], which, :, pl.ds(start + h * DH, DH)]
            for j, w in enumerate(weights)
        )

    def stat_lanes(overall, total):
        lane_id = lax.broadcasted_iota(jnp.int32, (rows, LANES), 1)
        packed = jnp.where(lane_id < HALF, overall, pltpu.roll(total, HALF, 1))
        return jnp.where(lane_id % HALF < GROUP, packed, 0.0)

    visual_back = []
    for s in range(seqs):
        def pair_step(g, carry, s=s):
            overall, total, weights = visual_weights(s, g, 1)
            inverse = 1.0 / jnp.where(total > 0.0, total, 1.0)
            weights = [w * inverse for w in weights]
            start = pl.multiple_of(g * (GROUP * DH), DH)
            for h in range(GROUP):
                v_send[s, :, pl.ds(start + h * DH, DH)] = weighted(s, g, 1, h, weights).astype(
                    jnp.bfloat16
                )
            v_stat_send[s] = v_stat_send[s] + pltpu.roll(stat_lanes(overall, total), g * 8, 1)
            return carry

        lax.fori_loop(0, groups, pair_step, 0)
        visual_back.append((
            send(v_send.at[s], v_recv.at[s], pair), send(v_stat_send.at[s], v_stat_recv.at[s], pair)
        ))

    attend_far(slot_of("diag", members - 1), here - 1, (0,))

    for piece in gates:
        piece.wait_recv()
    for s in range(seqs):
        logits = gate_own[s]
        for k in range(len(twins)):
            logits = logits + gate_recv[k, s]
        heads = groups * GROUP
        mine = logits[:, :heads]
        for c in range(1, heads_split):
            mine = jnp.where(core == c, logits[:, c * heads:(c + 1) * heads], mine)
        mine = jax.nn.sigmoid(mine)
        for g in range(groups):
            gate_buf[s, g, :, :GROUP] = mine[:, g * GROUP:(g + 1) * GROUP]

    for piece in text_back:
        piece.wait_recv()

    def unpacked(packed, g):
        return pltpu.roll(packed, LANES - g * 8, 1)

    def text_merge(i, carry):
        s, g = i // groups, i % groups
        ours, theirs = t_own_stat[s, g], unpacked(t_stat_recv[s], g)
        overall = jnp.maximum(ours, theirs)
        weight_a = jnp.exp(ours - overall)
        weight_b = jnp.exp(theirs - overall) * totals_of(theirs)
        inverse = 1.0 / (weight_a * totals_of(ours) + weight_b)
        weight_a, weight_b = weight_a * inverse, weight_b * inverse
        start = pl.multiple_of(g * (GROUP * DH), DH)
        for h in range(GROUP):
            cut = pl.ds(start + h * DH, DH)
            t_own[s, :, cut] = weight_a[:, h:h + 1] * t_own[s, :, cut] + weight_b[
                :, h:h + 1
            ] * t_recv[s, :, cut].astype(jnp.float32)
        return carry

    lax.fori_loop(0, seqs * groups, text_merge, 0)

    for s in range(seqs):
        for piece in visual_back[s]:
            piece.wait_recv()

        def own_step(g, carry, s=s):
            overall, total, weights = visual_weights(s, g, 0)
            theirs = unpacked(v_stat_recv[s], g)
            joint = jnp.maximum(overall, theirs)
            weight_a = jnp.exp(overall - joint)
            weight_b = jnp.exp(theirs - joint) * totals_of(theirs)
            inverse = 1.0 / (weight_a * total + weight_b)
            weights = [w * (weight_a * inverse) for w in weights]
            weight_b = weight_b * inverse
            start = pl.multiple_of(g * (GROUP * DH), DH)
            for h in range(GROUP):
                cut = pl.ds(start + h * DH, DH)
                visual = weighted(s, g, 0, h, weights) + weight_b[:, h:h + 1] * v_recv[
                    s, :, cut
                ].astype(jnp.float32)
                gate = gate_buf[s, g, :, h:h + 1]
                out_ref[s, :, cut] = ((1.0 - gate) * t_own[s, :, cut] + gate * visual).astype(
                    jnp.bfloat16
                )
            return carry

        lax.fori_loop(0, groups, own_step, 0)

    for copy in copies:
        copy.wait_send()


def on_device(n, heads_split, queries, text_keys, text_values, visual_keys, visual_values,
              gate_weight, text_offsets, image_sequence, image_position):
    seqs, rows, columns = queries.shape
    groups = text_keys.shape[-1] // DH
    here, tokens, kv_columns = visual_keys.shape
    members, blocks = n // 4, n // 2
    slots = blocks * here
    per_seq = image_sequence.shape[0] // seqs
    smem = pl.BlockSpec(memory_space=pltpu.SMEM)
    vmem = pl.BlockSpec(memory_space=pltpu.VMEM)
    bf16, f32 = jnp.bfloat16, jnp.float32
    count = 1 + 4 * (members - 1) + 2 + here * (2 * (members - 1) * (1 + len(chunks_of(tokens))) + 2) + 2 + 2 * seqs + heads_split - 1
    stats = (seqs, groups, rows, LANES)
    sent_stats = (seqs, rows, LANES)
    gate_shape = (seqs, rows, gate_weight.shape[-1])
    pairs = 2 * rows * GROUP * groups * (slots * tokens + seqs * blocks * rows)
    return pl.pallas_call(
        functools.partial(attention_kernel, n, heads_split, seqs, rows, groups, here, per_seq),
        in_specs=[smem] * 3 + [vmem] * 6,
        out_specs=vmem,
        out_shape=jax.ShapeDtypeStruct(queries.shape, bf16),
        scratch_shapes=[
            pltpu.VMEM(queries.shape, bf16),
            pltpu.VMEM((blocks - 1, *text_keys.shape), bf16),
            pltpu.VMEM((blocks - 1, *text_keys.shape), bf16),
            pltpu.VMEM((blocks - 1, *visual_keys.shape), bf16),
            pltpu.VMEM((blocks - 1, *visual_keys.shape), bf16),
            pltpu.VMEM((slots, 2, rows, columns), f32),
            pltpu.VMEM((slots, 2, groups, rows, LANES), f32),
            pltpu.VMEM((seqs, blocks * rows, kv_columns), bf16),
            pltpu.VMEM((seqs, blocks * rows, kv_columns), bf16),
            pltpu.VMEM(queries.shape, bf16),
            pltpu.VMEM(sent_stats, f32),
            pltpu.VMEM(queries.shape, bf16),
            pltpu.VMEM(sent_stats, f32),
            pltpu.VMEM(queries.shape, bf16),
            pltpu.VMEM(sent_stats, f32),
            pltpu.VMEM(queries.shape, bf16),
            pltpu.VMEM(sent_stats, f32),
            pltpu.VMEM(queries.shape, f32),
            pltpu.VMEM(stats, f32),
            pltpu.VMEM(gate_shape, f32),
            pltpu.VMEM((heads_split - 1, *gate_shape), f32),
            pltpu.VMEM(stats, f32),
            pltpu.SemaphoreType.DMA((count,)),
            pltpu.SemaphoreType.DMA((count,)),
        ],
        compiler_params=pltpu.CompilerParams(
            collective_id=0, has_side_effects=True, vmem_limit_bytes=60 << 20
        ),
        cost_estimate=pl.CostEstimate(
            flops=4 * pairs * DH, bytes_accessed=16 << 20, transcendentals=pairs
        ),
    )(
        text_offsets, image_sequence, image_position,
        queries, text_keys, text_values, visual_keys, visual_values, gate_weight.T,
    )


def solution(mesh):
    return jax.shard_map(
        functools.partial(on_device, mesh.shape["seq"], mesh.shape["kvh"]),
        mesh=mesh,
        in_specs=(
            P("batch", "seq", "kvh"),
            P("batch", "seq", "kvh"),
            P("batch", "seq", "kvh"),
            P(("batch", "seq"), None, "kvh"),
            P(("batch", "seq"), None, "kvh"),
            P("kvh", None),
            P("batch"),
            P("batch"),
            P("batch"),
        ),
        out_specs=P("batch", "seq", "kvh"),
        check_vma=False,
    )
```
